32 devices in a mesh: seq: 4 (over y, core), fsdp: 2 (over x), dp: 4 (over z).
Axes of the slice: x: 2, y: 2, z: 4, core: 2. Of those that a mesh axis runs over, the one named last changes fastest.
Arguments:
- queries: bfloat16 [8, 1024, 4096], P(('fsdp', 'dp'), 'seq'), may hold values from -160 to 160
- hidden: bfloat16 [8, 1024, 8192], P(('fsdp', 'dp'), 'seq'), may hold values from -8 to 8
- key_weight: bfloat16 [8192, 512], P('fsdp'), may hold values from -1 to 1
- doc_lengths: int32 [8, 8], P(('fsdp', 'dp')), may hold values from 1 to 256, 1024 in all within a row
- entropy_cot: bfloat16 [8, 1024, 32], P(('fsdp', 'dp'), 'seq'), may hold values from -600 to 600
Outputs:
- entropy: float32 [8, 1024, 32], P(('fsdp', 'dp'), 'seq')
- grad_queries: bfloat16 [8, 1024, 4096], P(('fsdp', 'dp'), 'seq')
- grad_key_weight: bfloat16 [8192, 512], P('fsdp')
The draws below stay inside these ranges and needn't reach their ends.
Inputs may be any that keep to these rules, and one draw needn't show every extreme that they name: `doc_lengths`: each sequence's 8 documents are packed in order, their lengths sum to 1024, and the longest is exactly 256.
All inputs are finite; a program needn't handle non-finite values.
Results may differ from the reference program's by a relative error of at most 0.0088.
Values may be sent and summed in bfloat16 or wider, within the bound.
A program may use at most 128 MiB of HBM per device.

```python
import math
import jax
import jax.numpy as jnp
import numpy as np
from jax import lax

D = 8192
QH = 32
KVH = 4
HD = 128
LENGTH = 1024
DOC = 256
NDOC = 8
SEQS = 8


def weight_values(key):
    values = jax.random.normal(jax.random.fold_in(key, 202), (D, KVH * HD), jnp.float32) * D ** (-0.5)
    return jnp.clip(values, -1.0, 1.0)


def hidden_values(key):
    values = jax.random.normal(jax.random.fold_in(key, 101), (SEQS, LENGTH, D), jnp.float32)
    return jnp.clip(values, -8.0, 8.0)


def draw_hidden(key, part):
    return hidden_values(key).astype(jnp.bfloat16)


def draw_key_weight(key, part):
    return weight_values(key).astype(jnp.bfloat16)


def draw_queries(key, part):
    values = jnp.clip(jax.random.normal(jax.random.fold_in(key, 303), (SEQS, LENGTH, QH * HD), jnp.float32), -6.0, 6.0)
    return values.astype(jnp.bfloat16)


def shard_levels(rng, extent, shards, least, high):
    gain, own = 1.0, jax.random.fold_in(rng, 6)
    for dim, parts in shards:
        draws = jnp.exp(jax.random.uniform(jax.random.fold_in(own, dim), (parts,), jnp.float32, least / len(shards), high / len(shards)))
        gain = gain * jnp.repeat(draws, extent[dim] // parts).reshape([-1 if axis == dim else 1 for axis in range(len(extent))])
    return gain


def split_up(number_of, total, most, lean):
    weights = [(1 << 20) // math.isqrt(standing ** lean) + 1 for standing in range(2, number_of + 1)]
    rest, holding = total - most - (number_of - 1), [1] * (number_of - 1)
    while rest > 0:
        free = [i for i in range(number_of - 1) if holding[i] < most]
        pool, remaining = sum([weights[i] for i in free]), rest
        for i in free:
            more = min(most - holding[i], max(1, remaining * weights[i] // pool), rest)
            holding[i] = holding[i] + more
            rest = rest - more
    return np.array([most] + holding)


def ragged(key, amount, total, reach, skew):
    if amount == 2:
        one = jax.random.randint(key, (), max(1, total - reach), min(reach, total - 1) + 1)
        return jnp.stack([one, total - one])
    sizes = jnp.asarray(split_up(amount, total, reach, skew), jnp.int32)
    pairs = (amount - 1) // 2
    donor, sink = sizes[1:1 + 2 * pairs:2], sizes[2:2 + 2 * pairs:2]
    margin = jnp.minimum(donor - 1, reach - sink)
    passed = jax.random.randint(jax.random.fold_in(key, 1), (pairs,), 0, 1 << 20) % (margin + 1)
    sizes = sizes.at[1:1 + 2 * pairs:2].set(donor - passed).at[2:2 + 2 * pairs:2].set(sink + passed)
    return sizes[jax.random.permutation(jax.random.fold_in(key, 2), amount)]


def normal_values(stream_key, extent, width, most, shards=(), kind=jnp.bfloat16):
    values = width * jax.random.normal(stream_key, extent, jnp.float32)
    if shards:
        values = values * shard_levels(stream_key, extent, shards, -0.22, 0.18)
    return jnp.clip(values, -most, most).astype(kind)


def setup_inputs(seed: int = 0) -> dict:
    keys = jax.random.split(jax.random.key(seed), 6)
    queries = draw_queries(jax.random.fold_in(keys[5], 71), 0)
    hidden = draw_hidden(jax.random.fold_in(keys[5], 71), 0)
    key_weight = draw_key_weight(jax.random.fold_in(keys[5], 71), 0)
    doc_lengths = jax.vmap(lambda own: ragged(own, NDOC, LENGTH, DOC, 1))(jax.random.split(keys[3], SEQS)).reshape((SEQS, NDOC)).astype(jnp.int32)
    entropy_cot = normal_values(keys[4], (SEQS, LENGTH, QH), 100.0, 600.0, ((0, 8), (1, 4)))
    return {"queries": queries, "hidden": hidden, "key_weight": key_weight, "doc_lengths": doc_lengths, "entropy_cot": entropy_cot}


def document_index(lengths, seq_len):
    ends = jnp.cumsum(lengths.astype(jnp.int32)).astype(jnp.int32)
    position = jnp.arange(seq_len, dtype=jnp.int32)
    return jnp.sum((ends[None, :] <= position[:, None]).astype(jnp.int32), axis=1).astype(jnp.int32)


def attend(queries, key_rows, cotangent, doc_index, anchor, doc_len):
    row_count, key_heads, group_size, head_size = queries.shape
    full_len = key_rows.shape[0]
    block_rows = min(512, row_count)
    window = block_rows + doc_len
    factor = head_size ** -0.5
    keys_padded = jnp.concatenate([jnp.zeros((doc_len, key_heads, head_size), key_rows.dtype), key_rows], axis=0)
    index_padded = jnp.concatenate([jnp.full((doc_len,), -1, jnp.int32), doc_index.astype(jnp.int32)], axis=0)

    def one_block(step_index, state_now):
        entropy, grad_query, grad_key = state_now
        row_start = (step_index * block_rows).astype(jnp.int32)
        position = (anchor + row_start).astype(jnp.int32)
        query_block = lax.dynamic_slice_in_dim(queries, row_start, block_rows, 0).astype(jnp.float32)
        weight_block = lax.dynamic_slice_in_dim(cotangent, row_start, block_rows, 0).astype(jnp.float32)
        key_block = lax.dynamic_slice_in_dim(keys_padded, position, window, 0).astype(jnp.float32)
        key_docs = lax.dynamic_slice_in_dim(index_padded, position, window, 0)
        query_docs = lax.dynamic_slice_in_dim(doc_index.astype(jnp.int32), position, block_rows, 0)
        query_pos = position + jnp.arange(block_rows, dtype=jnp.int32)
        key_pos = position - doc_len + jnp.arange(window, dtype=jnp.int32)
        visible = (query_docs[:, None] == key_docs[None, :]) & (key_pos[None, :] <= query_pos[:, None])
        scores = jnp.einsum("rkgd,wkd->kgrw", query_block, key_block, precision=lax.Precision.HIGHEST) * factor
        scores = jnp.where(visible, scores, -1e30)
        row_max = jnp.max(scores, axis=-1, keepdims=True)
        powers = jnp.exp(scores - row_max)
        denominator = jnp.sum(powers, axis=-1, keepdims=True)
        probability = powers / denominator
        mean_score = jnp.sum(jnp.where(visible, probability * scores, 0.0), axis=-1, keepdims=True)
        block_entropy = (row_max + jnp.log(denominator) - mean_score)[..., 0]
        row_weight = jnp.transpose(weight_block, (1, 2, 0))[..., None]
        slope = jnp.where(visible, row_weight * probability * (mean_score - scores), 0.0).astype(jnp.bfloat16)
        slope = lax.optimization_barrier(slope).astype(jnp.float32)
        query_part = jnp.einsum("kgrw,wkd->rkgd", slope, key_block, precision=lax.Precision.HIGHEST) * factor
        key_part = jnp.einsum("kgrw,rkgd->wkd", slope, query_block, precision=lax.Precision.HIGHEST) * factor
        entropy = lax.dynamic_update_slice_in_dim(entropy, jnp.transpose(block_entropy, (2, 0, 1)), row_start, 0)
        grad_query = lax.dynamic_update_slice_in_dim(grad_query, query_part, row_start, 0)
        previous = lax.dynamic_slice_in_dim(grad_key, position, window, 0)
        grad_key = lax.dynamic_update_slice_in_dim(grad_key, previous + key_part, position, 0)
        return entropy, grad_query, grad_key

    initial = (jnp.zeros((row_count, key_heads, group_size), jnp.float32),
               jnp.zeros((row_count, key_heads, group_size, head_size), jnp.float32),
               jnp.zeros((full_len + doc_len, key_heads, head_size), jnp.float32))
    entropy, grad_query, grad_key = lax.fori_loop(0, row_count // block_rows, one_block, initial)
    return entropy, grad_query, grad_key[doc_len:]


def reference(queries, hidden, key_weight, doc_lengths, entropy_cot):
    group_size = QH // KVH

    def one_sequence(items):
        query_rows, hidden_rows, lengths, cot_rows = items
        doc_index = document_index(lengths, LENGTH)
        key_rows = jnp.dot(hidden_rows, key_weight, preferred_element_type=jnp.float32).astype(jnp.bfloat16)
        key_rows = key_rows.reshape(LENGTH, KVH, HD)
        query_four = query_rows.reshape(LENGTH, KVH, group_size, HD)
        cot_three = cot_rows.reshape(LENGTH, KVH, group_size)
        outcome = [attend(query_four[:, head_index:head_index + 1], key_rows[:, head_index:head_index + 1],
                          cot_three[:, head_index:head_index + 1], doc_index, 0, DOC) for head_index in range(KVH)]
        entropy = jnp.concatenate([item_set[0] for item_set in outcome], axis=1).reshape(LENGTH, QH)
        grad_query = jnp.concatenate([item_set[1] for item_set in outcome], axis=1).reshape(LENGTH, QH * HD)
        key_grad = jnp.concatenate([item_set[2] for item_set in outcome], axis=1).reshape(LENGTH, KVH * HD)
        key_grad = key_grad.astype(jnp.bfloat16)
        weight_grad = jnp.dot(hidden_rows.T, key_grad, preferred_element_type=jnp.float32)
        return entropy, grad_query.astype(jnp.bfloat16), weight_grad

    entropy, grad_query, weight_grads = lax.map(one_sequence, (queries, hidden, doc_lengths, entropy_cot))
    weight_grad = jnp.sum(weight_grads, axis=0) * ((SEQS * LENGTH) ** -0.5)
    return entropy, grad_query, weight_grad.astype(jnp.bfloat16)
```

```python
import jax
import jax.numpy as jnp
from jax import lax
from jax.sharding import PartitionSpec as P

QH = 32
KVH = 4
HD = 128


def from_behind(shard, axis, by):
    length = lax.axis_size(axis)
    pairs = [(i, i + by) for i in range(length) if 0 <= i + by < length]
    return lax.ppermute(shard, axis, pairs)


def document_index(lengths, seq_len):
    ends = jnp.cumsum(lengths)
    position = jnp.arange(seq_len, dtype=jnp.int32)
    return jnp.sum((ends[None, :] <= position[:, None]).astype(jnp.int32), axis=1)


def attend(queries, key_rows, cotangent, doc_index, anchor, doc_len):
    row_count, key_heads, group_size, head_size = queries.shape
    full_len = key_rows.shape[0]
    block_rows = min(512, row_count)
    window = block_rows + doc_len
    factor = head_size ** (-0.5)
    keys_padded = jnp.concatenate(
        [jnp.zeros((doc_len, key_heads, head_size), key_rows.dtype), key_rows], axis=0
    )
    index_padded = jnp.concatenate([jnp.full((doc_len,), -1, jnp.int32), doc_index], axis=0)

    def one_block(step_index, state_now):
        entropy, grad_query, grad_key = state_now
        row_start = (step_index * block_rows).astype(jnp.int32)
        position = anchor + row_start
        weight_block = cotangent.astype(jnp.float32)
        key_block = lax.dynamic_slice_in_dim(keys_padded, position, window, 0)
        key_docs = lax.dynamic_slice_in_dim(index_padded, position, window, 0)
        query_docs = lax.dynamic_slice_in_dim(doc_index, position, block_rows, 0)
        query_pos = position + jnp.arange(block_rows, dtype=jnp.int32)
        key_pos = position - doc_len + jnp.arange(window, dtype=jnp.int32)
        visible = (query_docs[:, None] == key_docs[None, :]) & (
            key_pos[None, :] <= query_pos[:, None]
        )
        scores = (
            jnp.einsum("rkgd,wkd->kgrw", queries, key_block, preferred_element_type=jnp.float32)
            * factor
        )
        scores = jnp.where(visible, scores, -1e30)
        row_max = jnp.max(scores, axis=-1, keepdims=True)
        powers = jnp.exp(scores - row_max)
        denominator = jnp.sum(powers, axis=-1, keepdims=True)
        probability = powers / denominator
        mean_score = jnp.sum(jnp.where(visible, probability * scores, 0.0), axis=-1, keepdims=True)
        block_entropy = (row_max + jnp.log(denominator) - mean_score)[..., 0]
        row_weight = jnp.transpose(weight_block, (1, 2, 0))[..., None]
        slope = jnp.where(visible, row_weight * probability * (mean_score - scores), 0.0).astype(
            jnp.bfloat16
        )
        query_part = (
            jnp.einsum("kgrw,wkd->rkgd", slope, key_block, preferred_element_type=jnp.float32)
            * factor
        )
        key_part = (
            jnp.einsum("kgrw,rkgd->wkd", slope, queries, preferred_element_type=jnp.float32)
            * factor
        )
        entropy = jnp.transpose(block_entropy, (2, 0, 1))
        grad_query = query_part
        previous = lax.dynamic_slice_in_dim(grad_key, position, window, 0)
        grad_key = lax.dynamic_update_slice_in_dim(grad_key, previous + key_part, position, 0)
        return (entropy, grad_query, grad_key)

    initial = (
        jnp.zeros((row_count, key_heads, group_size), jnp.float32),
        jnp.zeros((row_count, key_heads, group_size, head_size), jnp.float32),
        jnp.zeros((full_len + doc_len, key_heads, head_size), jnp.float32),
    )
    entropy, grad_query, grad_key = lax.fori_loop(0, row_count // block_rows, one_block, initial)
    return (entropy, grad_query, grad_key[doc_len:])


def per_head(query_four, key_rows, cot_three, doc_index, anchor, doc_len):
    outcome = [
        attend(
            query_four[:, head_index : head_index + 1],
            key_rows[:, head_index : head_index + 1],
            cot_three[:, head_index : head_index + 1],
            doc_index,
            anchor,
            doc_len,
        )
        for head_index in range(query_four.shape[1])
    ]
    entropy = jnp.concatenate([item_set[0] for item_set in outcome], axis=1)
    grad_query = jnp.concatenate([item_set[1] for item_set in outcome], axis=1)
    grad_key = jnp.concatenate([item_set[2] for item_set in outcome], axis=1)
    return (entropy, grad_query, grad_key)


def after(value, *earlier):
    return lax.optimization_barrier((value, *earlier))[0]


def pair_count(seq_parts):
    return 2 if seq_parts % 2 == 0 else 1


def shift_seq(value, dy, dc):
    parts = lax.axis_size("seq")
    cores = pair_count(parts)
    chips = parts // cores
    pairs = [
        (y * cores + c, ((y + dy) % chips) * cores + (c ^ dc))
        for y in range(chips)
        for c in range(cores)
    ]
    return lax.ppermute(value, "seq", pairs)


def shift_axis(value, axis, by):
    parts = lax.axis_size(axis)
    return lax.ppermute(value, axis, [(i, (i + by) % parts) for i in range(parts)])


def shift_plane(value, df, dy, dc):
    fsdp, parts = lax.axis_size("fsdp"), lax.axis_size("seq")
    cores = pair_count(parts)
    chips = parts // cores
    pairs = [
        ((y * cores + c) * fsdp + f, (((y + dy) % chips) * cores + (c ^ dc)) * fsdp + (f + df) % fsdp)
        for f in range(fsdp)
        for y in range(chips)
        for c in range(cores)
    ]
    return lax.ppermute(value, ("seq", "fsdp"), pairs)


def shards(queries, hidden, key_weight, doc_lengths, entropy_cot):
    tokens = hidden[0]
    local_rows, width = tokens.shape
    seq_parts = lax.axis_size("seq")
    fsdp_parts = lax.axis_size("fsdp")
    dp_parts = lax.axis_size("dp")
    cores = pair_count(seq_parts)
    chips = seq_parts // cores
    f_pos, s_pos, z_pos = lax.axis_index("fsdp"), lax.axis_index("seq"), lax.axis_index("dp")
    y_pos, c_pos = s_pos // cores, s_pos % cores
    shard_rows = width // fsdp_parts
    slab = shard_rows // seq_parts
    seq_len = local_rows * seq_parts
    group_size = QH // KVH
    doc_index = document_index(doc_lengths[0], seq_len)

    def seq_at(dy, dc):
        return ((y_pos + dy) % chips) * cores + (c_pos ^ dc)

    def column_slab(f, s, start, count):
        return lax.dynamic_slice_in_dim(tokens, f * shard_rows + s * slab + start, count, 1)

    own_piece = lax.dynamic_slice_in_dim(key_weight, s_pos * slab, slab, 0)
    chunks = 4
    chunk = slab // chunks
    arrived = []
    for df in range(1, fsdp_parts):
        for k in range(chunks):
            arrived.append((df, k, shift_axis(own_piece[k * chunk : (k + 1) * chunk], "fsdp", df)))
    key_sum = jnp.dot(
        lax.dynamic_slice_in_dim(tokens, f_pos * shard_rows, shard_rows, 1),
        key_weight,
        preferred_element_type=jnp.float32,
    )
    for df, k, piece in arrived:
        for dy in range(chips):
            along = piece if dy == 0 else shift_seq(piece, dy, 0)
            for dc in range(cores):
                block = along if dc == 0 else shift_seq(along, 0, dc)
                columns = column_slab((f_pos - df) % fsdp_parts, seq_at(-dy, dc), k * chunk, chunk)
                key_sum = key_sum + jnp.dot(columns, block, preferred_element_type=jnp.float32)
    key_local = key_sum.astype(jnp.bfloat16)

    plane = [
        (df, dy, dc) for df in range(fsdp_parts) for dy in range(chips) for dc in range(cores)
    ]
    gate = [item[2] for item in arrived]
    token_blocks = []
    for df, dy, dc in plane:
        block = column_slab((f_pos + df) % fsdp_parts, seq_at(dy, dc), 0, slab)
        if (df, dy, dc) != (0, 0, 0):
            if gate:
                block = after(block, gate[-1])
            block = shift_plane(block, df, dy, dc)
        token_blocks.append(block)

    query_local = queries[0]
    cot_local = entropy_cot[0]
    key_prev = from_behind(key_local, "seq", 1)
    start = s_pos * local_rows
    prev_index = lax.dynamic_slice_in_dim(
        doc_index, jnp.maximum(start - local_rows, 0), local_rows, 0
    )
    prev_index = jnp.where(s_pos > 0, prev_index, -1)
    own_index = lax.dynamic_slice_in_dim(doc_index, start, local_rows, 0)
    ext_index = jnp.concatenate([prev_index, own_index], axis=0)
    ext_keys = jnp.concatenate([key_prev, key_local], axis=0).reshape(2 * local_rows, KVH, HD)
    entropy_heads, grad_heads, key_heads_ext = per_head(
        query_local.reshape(local_rows, KVH, group_size, HD),
        ext_keys,
        cot_local.reshape(local_rows, KVH, group_size),
        ext_index,
        local_rows,
        local_rows,
    )
    entropy_local = entropy_heads.reshape(local_rows, QH)
    grad_local = grad_heads.reshape(local_rows, QH * HD)
    key_ext = key_heads_ext.reshape(2 * local_rows, KVH * HD)
    returned = from_behind(key_ext[:local_rows], "seq", -1)
    key_grad = (key_ext[local_rows:] + returned).astype(jnp.bfloat16)

    token_blocks = [after(block, key_grad) for block in token_blocks]

    held = {(0, 0): key_grad}
    for df in range(1, fsdp_parts):
        held[(df, 0)] = shift_axis(key_grad, "fsdp", df)
    for df in range(fsdp_parts):
        for dy in range(1, chips):
            held[(df, dy)] = shift_seq(held[(df, 0)], dy, 0)
    key_blocks = [
        held[(df, dy)] if dc == 0 else shift_seq(held[(df, dy)], 0, dc) for df, dy, dc in plane
    ]
    term = lax.dot_general(
        jnp.concatenate(token_blocks, axis=0),
        jnp.concatenate(key_blocks, axis=0),
        (((0,), (0,)), ((), ())),
        preferred_element_type=jnp.float32,
    )

    share = slab // dp_parts
    total = lax.dynamic_slice_in_dim(term, z_pos * share, share, 0)
    for dz in range(1, dp_parts):
        part = lax.dynamic_slice_in_dim(term, ((z_pos + dz) % dp_parts) * share, share, 0)
        total = total + shift_axis(part.astype(jnp.bfloat16), "dp", dz).astype(jnp.float32)
    norm_factor = (seq_len * fsdp_parts * dp_parts) ** (-0.5)
    final = (total * norm_factor).astype(jnp.bfloat16)

    weight_grad = jnp.zeros((shard_rows, final.shape[1]), jnp.bfloat16)
    for dz in range(dp_parts):
        along_z = final if dz == 0 else shift_axis(final, "dp", dz)
        for dy in range(chips):
            along = along_z if dy == 0 else shift_seq(along_z, dy, 0)
            for dc in range(cores):
                block = along if dc == 0 else shift_seq(along, 0, dc)
                row = seq_at(-dy, dc) * slab + ((z_pos - dz) % dp_parts) * share
                weight_grad = lax.dynamic_update_slice_in_dim(weight_grad, block, row, 0)
    return (
        entropy_local.reshape(1, local_rows, QH),
        grad_local.astype(jnp.bfloat16).reshape(1, local_rows, QH * HD),
        weight_grad,
    )


def solution(mesh):
    return jax.shard_map(
        shards,
        mesh=mesh,
        in_specs=(
            P(("fsdp", "dp"), "seq", None),
            P(("fsdp", "dp"), "seq", None),
            P("fsdp", None),
            P(("fsdp", "dp"), None),
            P(("fsdp", "dp"), "seq", None),
        ),
        out_specs=(P(("fsdp", "dp"), "seq", None), P(("fsdp", "dp"), "seq", None), P("fsdp", None)),
        check_vma=False,
    )
```

```python
import functools

import jax
import jax.numpy as jnp
from jax import lax
from jax.experimental import pallas as pl
from jax.experimental.pallas import tpu as pltpu
from jax.sharding import PartitionSpec as P

QH = 32
KVH = 4
HD = 128


def from_behind(shard, axis, by):
    length = lax.axis_size(axis)
    pairs = [(i, i + by) for i in range(length) if 0 <= i + by < length]
    return lax.ppermute(shard, axis, pairs)


def document_index(lengths, seq_len):
    ends = jnp.cumsum(lengths)
    position = jnp.arange(seq_len, dtype=jnp.int32)
    return jnp.sum((ends[None, :] <= position[:, None]).astype(jnp.int32), axis=1)


def attend(queries, key_rows, cotangent, doc_index, anchor, doc_len):
    row_count, key_heads, group_size, head_size = queries.shape
    full_len = key_rows.shape[0]
    block_rows = min(512, row_count)
    window = block_rows + doc_len
    factor = head_size ** (-0.5)
    keys_padded = jnp.concatenate(
        [jnp.zeros((doc_len, key_heads, head_size), key_rows.dtype), key_rows], axis=0
    )
    index_padded = jnp.concatenate([jnp.full((doc_len,), -1, jnp.int32), doc_index], axis=0)

    def one_block(step_index, state_now):
        entropy, grad_query, grad_key = state_now
        row_start = (step_index * block_rows).astype(jnp.int32)
        position = anchor + row_start
        weight_block = cotangent.astype(jnp.float32)
        key_block = lax.dynamic_slice_in_dim(keys_padded, position, window, 0)
        key_docs = lax.dynamic_slice_in_dim(index_padded, position, window, 0)
        query_docs = lax.dynamic_slice_in_dim(doc_index, position, block_rows, 0)
        query_pos = position + jnp.arange(block_rows, dtype=jnp.int32)
        key_pos = position - doc_len + jnp.arange(window, dtype=jnp.int32)
        visible = (query_docs[:, None] == key_docs[None, :]) & (
            key_pos[None, :] <= query_pos[:, None]
        )
        scores = (
            jnp.einsum("rkgd,wkd->kgrw", queries, key_block, preferred_element_type=jnp.float32)
            * factor
        )
        scores = jnp.where(visible, scores, -1e30)
        row_max = jnp.max(scores, axis=-1, keepdims=True)
        powers = jnp.exp(scores - row_max)
        denominator = jnp.sum(powers, axis=-1, keepdims=True)
        probability = powers / denominator
        mean_score = jnp.sum(jnp.where(visible, probability * scores, 0.0), axis=-1, keepdims=True)
        block_entropy = (row_max + jnp.log(denominator) - mean_score)[..., 0]
        row_weight = jnp.transpose(weight_block, (1, 2, 0))[..., None]
        slope = jnp.where(visible, row_weight * probability * (mean_score - scores), 0.0).astype(
            jnp.bfloat16
        )
        query_part = (
            jnp.einsum("kgrw,wkd->rkgd", slope, key_block, preferred_element_type=jnp.float32)
            * factor
        )
        key_part = (
            jnp.einsum("kgrw,rkgd->wkd", slope, queries, preferred_element_type=jnp.float32)
            * factor
        )
        entropy = jnp.transpose(block_entropy, (2, 0, 1))
        grad_query = query_part
        previous = lax.dynamic_slice_in_dim(grad_key, position, window, 0)
        grad_key = lax.dynamic_update_slice_in_dim(grad_key, previous + key_part, position, 0)
        return (entropy, grad_query, grad_key)

    initial = (
        jnp.zeros((row_count, key_heads, group_size), jnp.float32),
        jnp.zeros((row_count, key_heads, group_size, head_size), jnp.float32),
        jnp.zeros((full_len + doc_len, key_heads, head_size), jnp.float32),
    )
    entropy, grad_query, grad_key = lax.fori_loop(0, row_count // block_rows, one_block, initial)
    return (entropy, grad_query, grad_key[doc_len:])


def per_head(query_four, key_rows, cot_three, doc_index, anchor, doc_len):
    outcome = [
        attend(
            query_four[:, head_index : head_index + 1],
            key_rows[:, head_index : head_index + 1],
            cot_three[:, head_index : head_index + 1],
            doc_index,
            anchor,
            doc_len,
        )
        for head_index in range(query_four.shape[1])
    ]
    entropy = jnp.concatenate([item_set[0] for item_set in outcome], axis=1)
    grad_query = jnp.concatenate([item_set[1] for item_set in outcome], axis=1)
    grad_key = jnp.concatenate([item_set[2] for item_set in outcome], axis=1)
    return (entropy, grad_query, grad_key)


def after(value, *earlier):
    return lax.optimization_barrier((value, *earlier))[0]


def pair_count(seq_parts):
    return 2 if seq_parts % 2 == 0 else 1


def shift_seq(value, dy, dc):
    parts = lax.axis_size("seq")
    cores = pair_count(parts)
    chips = parts // cores
    pairs = [
        (y * cores + c, ((y + dy) % chips) * cores + (c ^ dc))
        for y in range(chips)
        for c in range(cores)
    ]
    return lax.ppermute(value, "seq", pairs)


def shift_axis(value, axis, by):
    parts = lax.axis_size(axis)
    return lax.ppermute(value, axis, [(i, (i + by) % parts) for i in range(parts)])


def shift_plane(value, df, dy, dc):
    fsdp, parts = lax.axis_size("fsdp"), lax.axis_size("seq")
    cores = pair_count(parts)
    chips = parts // cores
    pairs = [
        ((y * cores + c) * fsdp + f, (((y + dy) % chips) * cores + (c ^ dc)) * fsdp + (f + df) % fsdp)
        for f in range(fsdp)
        for y in range(chips)
        for c in range(cores)
    ]
    return lax.ppermute(value, ("seq", "fsdp"), pairs)


MESH = pl.DeviceIdType.MESH


def tail_kernel(fsdp, chips, cores, depth, share, norm, *refs):
    count = fsdp * chips * cores
    key_ref, token_refs, out_ref = refs[0], refs[1 : 1 + count], refs[1 + count]
    held, acc, parts, landed, final, send, recv, local = refs[2 + count :]
    slab = depth * share
    f, s, z = lax.axis_index("fsdp"), lax.axis_index("seq"), lax.axis_index("dp")
    y, c = lax.div(s, cores), lax.rem(s, cores)

    def seq_at(dy, dc):
        other = c if dc == 0 else 1 - c
        return {"seq": lax.rem(y + dy + chips, chips) * cores + other}

    def fsdp_at(df):
        return {"fsdp": lax.rem(f + df, fsdp)}

    partners = [fsdp_at(df) for df in range(1, fsdp)]
    partners += [seq_at(dy, 0) for dy in range(1, chips)]
    partners += [seq_at(0, 1)] * (cores - 1)
    partners += [{"dp": lax.rem(z + dz, depth)} for dz in range(1, depth)]
    barrier = pltpu.get_barrier_semaphore()
    for device in partners:
        pl.semaphore_signal(barrier, inc=1, device_id=device, device_id_type=MESH)
    pl.semaphore_wait(barrier, len(partners))

    numbers = {}

    def remote(name, src, dst, device):
        slot = numbers.setdefault(name, len(numbers))
        return pltpu.make_async_remote_copy(
            src_ref=src,
            dst_ref=dst,
            send_sem=send.at[slot],
            recv_sem=recv.at[slot],
            device_id=device,
            device_id_type=MESH,
        )

    def place(df, dy, dc):
        return (df * chips + dy) * cores + dc

    def plane_copy(df, dy, dc):
        if dc:
            source, device = (df, dy, 0), seq_at(0, 1)
        elif dy:
            source, device = (df, 0, 0), seq_at(dy, 0)
        else:
            source, device = (0, 0, 0), fsdp_at(df)
        src = key_ref if source == (0, 0, 0) else held.at[place(*source)]
        return remote(("key", df, dy, dc), src, held.at[place(df, dy, dc)], device)

    def follow(df, dy, dc):
        if dc == 0:
            if dy == 0:
                for step in range(1, chips):
                    plane_copy(df, step, 0).start()
            if cores == 2:
                plane_copy(df, dy, 1).start()

    tile = min(256, slab)

    def accumulate(df, dy, dc):
        number = place(df, dy, dc)
        token_ref = token_refs[number]
        rows_ref = key_ref if number == 0 else held.at[number]

        @pl.loop(0, slab // tile)
        def _(step):
            at = pl.ds(pl.multiple_of(step * tile, tile), tile)
            value = lax.dot_general(
                token_ref[:, at], rows_ref[...], (((0,), (0,)), ((), ())),
                preferred_element_type=jnp.float32,
            )
            if number == 0:
                acc[at, :] = value
            else:
                acc[at, :] += value

    for df in range(1, fsdp):
        plane_copy(df, 0, 0).start()
    follow(0, 0, 0)
    accumulate(0, 0, 0)
    near = [(0, dy, 0) for dy in range(1, chips)] + [(df, 0, 0) for df in range(1, fsdp)]
    far = [(df, dy, 0) for df in range(1, fsdp) for dy in range(1, chips)]
    last = [(df, dy, 1) for df in range(fsdp) for dy in range(chips) if cores == 2]
    for group in (near, last[:1], far, last[1:]):
        for item in group:
            plane_copy(*item).wait_recv()
            follow(*item)
        for item in group:
            accumulate(*item)

    def part_copy(dz):
        return remote(
            ("part", dz), parts.at[dz - 1], landed.at[dz - 1], {"dp": lax.rem(z + dz, depth)}
        )

    for dz in range(1, depth):
        row = pl.multiple_of(lax.rem(z + dz, depth) * share, share)
        parts[dz - 1] = acc[pl.ds(row, share), :].astype(jnp.bfloat16)
        part_copy(dz).start()
    total = acc[pl.ds(pl.multiple_of(z * share, share), share), :]
    for dz in range(1, depth):
        part_copy(dz).wait_recv()
        total = total + landed[dz - 1].astype(jnp.float32)
    final[...] = (total * norm).astype(jnp.bfloat16)

    def rows(dy, dc, zz):
        chip = lax.rem(y - dy + chips, chips)
        core = c if dc == 0 else 1 - c
        row = ((chip * cores + core) * depth + zz) * share
        return out_ref.at[pl.ds(pl.multiple_of(row, share), share)]

    def event_depth(event):
        way, step = event
        return z if way == 0 else z - way * (step + 1)

    def event_live(event):
        where = event_depth(event)
        return (where >= 0) & (where < depth)

    def block_of(event):
        return final if event[0] == 0 else rows(0, 0, event_depth(event))

    def depth_copy(event):
        way, step = event
        where = z - way * step
        src = final if step == 0 else rows(0, 0, where)
        return remote(("z", event), src, rows(0, 0, where), {"dp": z + way})

    def depth_live(event):
        way, step = event
        where = z - way * step
        return (where >= 0) & (where < depth) & (z + way >= 0) & (z + way < depth)

    def row_copy(event, dy, dc):
        where = event_depth(event)
        if dc:
            return remote(
                ("c", event, dy), rows(dy, 0, where) if dy else block_of(event),
                rows(dy, 0, where), seq_at(0, 1),
            )
        return remote(("y", event, dy), block_of(event), rows(0, 0, where), seq_at(dy, 0))

    own = (0, 0)
    events = [own] + [(way, step) for step in range(depth - 1) for way in (1, -1)]
    own_copy = pltpu.make_async_copy(final, rows(0, 0, z), local)
    own_copy.start()

    def when(event, live, action):
        if event == own:
            action()
        else:
            pl.when(live(event))(action)

    def spread(event):
        for dy in range(1, chips):
            row_copy(event, dy, 0).start()
        if cores == 2:
            row_copy(event, 0, 1).start()

    def arrive(event):
        if event != own:
            depth_copy(event).wait_recv()
        spread(event)

    def relay(event):
        for dy in range(1, chips):
            row_copy(event, dy, 0).wait_recv()
            if cores == 2:
                row_copy(event, dy, 1).start()

    def close(event):
        for dy in range(1, chips):
            row_copy(event, dy, 0).wait_send()
        if cores == 2:
            for dy in range(chips):
                row_copy(event, dy, 1).wait()

    for way in (1, -1):
        if depth > 1:
            when((way, 0), depth_live, lambda way=way: depth_copy((way, 0)).start())
    before = None
    for event in events:
        when(event, event_live, functools.partial(arrive, event))
        if event != own and event[1] + 1 < depth - 1:
            after_it = (event[0], event[1] + 1)
            when(after_it, depth_live, lambda after_it=after_it: depth_copy(after_it).start())
        if before is not None:
            when(before, event_live, functools.partial(relay, before))
        before = event
    when(before, event_live, functools.partial(relay, before))
    for event in events:
        when(event, event_live, functools.partial(close, event))
        if event != own:
            when(event, depth_live, lambda event=event: depth_copy(event).wait_send())
    own_copy.wait()
    for df in range(fsdp):
        for dy in range(chips):
            for dc in range(cores):
                if (df, dy, dc) != (0, 0, 0):
                    plane_copy(df, dy, dc).wait_send()
    for dz in range(1, depth):
        part_copy(dz).wait_send()


def tail(key_grad, token_blocks, norm):
    fsdp, parts, depth = lax.axis_size("fsdp"), lax.axis_size("seq"), lax.axis_size("dp")
    cores = pair_count(parts)
    chips = parts // cores
    count = len(token_blocks)
    rows, slab = token_blocks[0].shape
    width = key_grad.shape[1]
    share = slab // depth
    copies = count - 1 + depth - 1 + 2 * (depth - 1) + (2 * depth - 1) * (chips - 1 + chips)
    return pl.pallas_call(
        functools.partial(tail_kernel, fsdp, chips, cores, depth, share, norm),
        out_shape=jax.ShapeDtypeStruct((slab * parts, width), jnp.bfloat16),
        in_specs=[pl.BlockSpec(memory_space=pltpu.VMEM)] * (1 + count),
        out_specs=pl.BlockSpec(memory_space=pl.ANY),
        scratch_shapes=[
            pltpu.VMEM((count, rows, width), jnp.bfloat16),
            pltpu.VMEM((slab, width), jnp.float32),
            pltpu.VMEM((max(depth - 1, 1), share, width), jnp.bfloat16),
            pltpu.VMEM((max(depth - 1, 1), share, width), jnp.bfloat16),
            pltpu.VMEM((share, width), jnp.bfloat16),
            pltpu.SemaphoreType.DMA((copies,)),
            pltpu.SemaphoreType.DMA((copies,)),
            pltpu.SemaphoreType.DMA(()),
        ],
        compiler_params=pltpu.CompilerParams(collective_id=0, has_side_effects=True),
        name="tail",
    )(key_grad, *token_blocks)


def shards(queries, hidden, key_weight, doc_lengths, entropy_cot):
    tokens = hidden[0]
    local_rows, width = tokens.shape
    seq_parts = lax.axis_size("seq")
    fsdp_parts = lax.axis_size("fsdp")
    dp_parts = lax.axis_size("dp")
    cores = pair_count(seq_parts)
    chips = seq_parts // cores
    f_pos, s_pos, z_pos = lax.axis_index("fsdp"), lax.axis_index("seq"), lax.axis_index("dp")
    y_pos, c_pos = s_pos // cores, s_pos % cores
    shard_rows = width // fsdp_parts
    slab = shard_rows // seq_parts
    seq_len = local_rows * seq_parts
    group_size = QH // KVH
    doc_index = document_index(doc_lengths[0], seq_len)

    def seq_at(dy, dc):
        return ((y_pos + dy) % chips) * cores + (c_pos ^ dc)

    def column_slab(f, s, start, count):
        return lax.dynamic_slice_in_dim(tokens, f * shard_rows + s * slab + start, count, 1)

    own_piece = lax.dynamic_slice_in_dim(key_weight, s_pos * slab, slab, 0)
    chunks = 4
    chunk = slab // chunks
    arrived = []
    for df in range(1, fsdp_parts):
        for k in range(chunks):
            arrived.append((df, k, shift_axis(own_piece[k * chunk : (k + 1) * chunk], "fsdp", df)))
    key_sum = jnp.dot(
        lax.dynamic_slice_in_dim(tokens, f_pos * shard_rows, shard_rows, 1),
        key_weight,
        preferred_element_type=jnp.float32,
    )
    for df, k, piece in arrived:
        for dy in range(chips):
            along = piece if dy == 0 else shift_seq(piece, dy, 0)
            for dc in range(cores):
                block = along if dc == 0 else shift_seq(along, 0, dc)
                columns = column_slab((f_pos - df) % fsdp_parts, seq_at(-dy, dc), k * chunk, chunk)
                key_sum = key_sum + jnp.dot(columns, block, preferred_element_type=jnp.float32)
    key_local = key_sum.astype(jnp.bfloat16)

    plane = [
        (df, dy, dc) for df in range(fsdp_parts) for dy in range(chips) for dc in range(cores)
    ]
    gate = [item[2] for item in arrived]
    token_blocks = []
    for df, dy, dc in plane:
        block = column_slab((f_pos + df) % fsdp_parts, seq_at(dy, dc), 0, slab)
        if (df, dy, dc) != (0, 0, 0):
            if gate:
                block = after(block, gate[-1])
            block = shift_plane(block, df, dy, dc)
        token_blocks.append(block)

    query_local = queries[0]
    cot_local = entropy_cot[0]
    key_prev = from_behind(key_local, "seq", 1)
    start = s_pos * local_rows
    prev_index = lax.dynamic_slice_in_dim(
        doc_index, jnp.maximum(start - local_rows, 0), local_rows, 0
    )
    prev_index = jnp.where(s_pos > 0, prev_index, -1)
    own_index = lax.dynamic_slice_in_dim(doc_index, start, local_rows, 0)
    ext_index = jnp.concatenate([prev_index, own_index], axis=0)
    ext_keys = jnp.concatenate([key_prev, key_local], axis=0).reshape(2 * local_rows, KVH, HD)
    entropy_heads, grad_heads, key_heads_ext = per_head(
        query_local.reshape(local_rows, KVH, group_size, HD),
        ext_keys,
        cot_local.reshape(local_rows, KVH, group_size),
        ext_index,
        local_rows,
        local_rows,
    )
    entropy_local = entropy_heads.reshape(local_rows, QH)
    grad_local = grad_heads.reshape(local_rows, QH * HD)
    key_ext = key_heads_ext.reshape(2 * local_rows, KVH * HD)
    returned = from_behind(key_ext[:local_rows], "seq", -1)
    key_grad = (key_ext[local_rows:] + returned).astype(jnp.bfloat16)

    token_blocks = [after(block, key_grad) for block in token_blocks]

    norm_factor = (seq_len * fsdp_parts * dp_parts) ** (-0.5)
    grad_local = grad_local.astype(jnp.bfloat16)
    key_grad, entropy_local, grad_local = lax.optimization_barrier(
        (key_grad, entropy_local, grad_local)
    )
    weight_grad = tail(key_grad, token_blocks, norm_factor)
    return (
        entropy_local.reshape(1, local_rows, QH),
        grad_local.reshape(1, local_rows, QH * HD),
        weight_grad,
    )


def solution(mesh):
    return jax.shard_map(
        shards,
        mesh=mesh,
        in_specs=(
            P(("fsdp", "dp"), "seq", None),
            P(("fsdp", "dp"), "seq", None),
            P("fsdp", None),
            P(("fsdp", "dp"), None),
            P(("fsdp", "dp"), "seq", None),
        ),
        out_specs=(P(("fsdp", "dp"), "seq", None), P(("fsdp", "dp"), "seq", None), P("fsdp", None)),
        check_vma=False,
    )
```

```python
import functools

import jax
import jax.numpy as jnp
from jax import lax
from jax.experimental import pallas as pl
from jax.experimental.pallas import tpu as pltpu
from jax.sharding import PartitionSpec as P


QH = 32
KVH = 4
HD = 128


def from_behind(shard, axis, by):
    length = lax.axis_size(axis)
    pairs = [(i, i + by) for i in range(length) if 0 <= i + by < length]
    return lax.ppermute(shard, axis, pairs)


def document_index(lengths, seq_len):
    ends = jnp.cumsum(lengths)
    position = jnp.arange(seq_len, dtype=jnp.int32)
    return jnp.sum((ends[None, :] <= position[:, None]).astype(jnp.int32), axis=1)


def attend(queries, key_rows, cotangent, doc_index, anchor, doc_len):
    row_count, key_heads, group_size, head_size = queries.shape
    full_len = key_rows.shape[0]
    block_rows = min(512, row_count)
    window = block_rows + doc_len
    factor = head_size ** (-0.5)
    keys_padded = jnp.concatenate(
        [jnp.zeros((doc_len, key_heads, head_size), key_rows.dtype), key_rows], axis=0
    )
    index_padded = jnp.concatenate([jnp.full((doc_len,), -1, jnp.int32), doc_index], axis=0)

    def one_block(step_index, state_now):
        entropy, grad_query, grad_key = state_now
        row_start = (step_index * block_rows).astype(jnp.int32)
        position = anchor + row_start
        weight_block = cotangent.astype(jnp.float32)
        key_block = lax.dynamic_slice_in_dim(keys_padded, position, window, 0)
        key_docs = lax.dynamic_slice_in_dim(index_padded, position, window, 0)
        query_docs = lax.dynamic_slice_in_dim(doc_index, position, block_rows, 0)
        query_pos = position + jnp.arange(block_rows, dtype=jnp.int32)
        key_pos = position - doc_len + jnp.arange(window, dtype=jnp.int32)
        visible = (query_docs[:, None] == key_docs[None, :]) & (
            key_pos[None, :] <= query_pos[:, None]
        )
        scores = (
            jnp.einsum("rkgd,wkd->kgrw", queries, key_block, preferred_element_type=jnp.float32)
            * factor
        )
        scores = jnp.where(visible, scores, -1e30)
        row_max = jnp.max(scores, axis=-1, keepdims=True)
        powers = jnp.exp(scores - row_max)
        denominator = jnp.sum(powers, axis=-1, keepdims=True)
        probability = powers / denominator
        mean_score = jnp.sum(jnp.where(visible, probability * scores, 0.0), axis=-1, keepdims=True)
        block_entropy = (row_max + jnp.log(denominator) - mean_score)[..., 0]
        row_weight = jnp.transpose(weight_block, (1, 2, 0))[..., None]
        slope = jnp.where(visible, row_weight * probability * (mean_score - scores), 0.0).astype(
            jnp.bfloat16
        )
        query_part = (
            jnp.einsum("kgrw,wkd->rkgd", slope, key_block, preferred_element_type=jnp.float32)
            * factor
        )
        key_part = (
            jnp.einsum("kgrw,rkgd->wkd", slope, queries, preferred_element_type=jnp.float32)
            * factor
        )
        entropy = jnp.transpose(block_entropy, (2, 0, 1))
        grad_query = query_part
        previous = lax.dynamic_slice_in_dim(grad_key, position, window, 0)
        grad_key = lax.dynamic_update_slice_in_dim(grad_key, previous + key_part, position, 0)
        return (entropy, grad_query, grad_key)

    initial = (
        jnp.zeros((row_count, key_heads, group_size), jnp.float32),
        jnp.zeros((row_count, key_heads, group_size, head_size), jnp.float32),
        jnp.zeros((full_len + doc_len, key_heads, head_size), jnp.float32),
    )
    entropy, grad_query, grad_key = lax.fori_loop(0, row_count // block_rows, one_block, initial)
    return (entropy, grad_query, grad_key[doc_len:])


def per_head(query_four, key_rows, cot_three, doc_index, anchor, doc_len):
    outcome = [
        attend(
            query_four[:, head_index : head_index + 1],
            key_rows[:, head_index : head_index + 1],
            cot_three[:, head_index : head_index + 1],
            doc_index,
            anchor,
            doc_len,
        )
        for head_index in range(query_four.shape[1])
    ]
    entropy = jnp.concatenate([item_set[0] for item_set in outcome], axis=1)
    grad_query = jnp.concatenate([item_set[1] for item_set in outcome], axis=1)
    grad_key = jnp.concatenate([item_set[2] for item_set in outcome], axis=1)
    return (entropy, grad_query, grad_key)


def after(value, *earlier):
    return lax.optimization_barrier((value, *earlier))[0]


def pair_count(seq_parts):
    return 2 if seq_parts % 2 == 0 else 1


def shift_plane(value, df, dy, dc):
    fsdp, parts = lax.axis_size("fsdp"), lax.axis_size("seq")
    cores = pair_count(parts)
    chips = parts // cores
    pairs = [
        ((y * cores + c) * fsdp + f, (((y + dy) % chips) * cores + (c ^ dc)) * fsdp + (f + df) % fsdp)
        for f in range(fsdp)
        for y in range(chips)
        for c in range(cores)
    ]
    return lax.ppermute(value, ("seq", "fsdp"), pairs)


MESH = pl.DeviceIdType.MESH


def tail_kernel(fsdp, chips, cores, depth, share, norm, *refs):
    count = fsdp * chips * cores
    key_ref, token_refs, out_ref = refs[0], refs[1 : 1 + count], refs[1 + count]
    held, acc, parts, landed, final, send, recv, local = refs[2 + count :]
    slab = depth * share
    f, s, z = lax.axis_index("fsdp"), lax.axis_index("seq"), lax.axis_index("dp")
    y, c = lax.div(s, cores), lax.rem(s, cores)

    def seq_at(dy, dc):
        other = c if dc == 0 else 1 - c
        return {"seq": lax.rem(y + dy + chips, chips) * cores + other}

    def fsdp_at(df):
        return {"fsdp": lax.rem(f + df, fsdp)}

    partners = [fsdp_at(df) for df in range(1, fsdp)]
    partners += [seq_at(dy, 0) for dy in range(1, chips)]
    partners += [seq_at(0, 1)] * (cores - 1)
    partners += [{"dp": lax.rem(z + dz, depth)} for dz in range(1, depth)]
    barrier = pltpu.get_barrier_semaphore()
    for device in partners:
        pl.semaphore_signal(barrier, inc=1, device_id=device, device_id_type=MESH)
    pl.semaphore_wait(barrier, len(partners))

    numbers = {}

    def remote(name, src, dst, device):
        slot = numbers.setdefault(name, len(numbers))
        return pltpu.make_async_remote_copy(
            src_ref=src,
            dst_ref=dst,
            send_sem=send.at[slot],
            recv_sem=recv.at[slot],
            device_id=device,
            device_id_type=MESH,
        )

    def place(df, dy, dc):
        return (df * chips + dy) * cores + dc

    def plane_copy(df, dy, dc):
        if dc:
            source, device = (df, dy, 0), seq_at(0, 1)
        elif dy:
            source, device = (df, 0, 0), seq_at(dy, 0)
        else:
            source, device = (0, 0, 0), fsdp_at(df)
        src = key_ref if source == (0, 0, 0) else held.at[place(*source)]
        return remote(("key", df, dy, dc), src, held.at[place(df, dy, dc)], device)

    def follow(df, dy, dc):
        if dc == 0:
            if dy == 0:
                for step in range(1, chips):
                    plane_copy(df, step, 0).start()
            if cores == 2:
                plane_copy(df, dy, 1).start()

    tile = min(256, slab)

    def accumulate(df, dy, dc):
        number = place(df, dy, dc)
        token_ref = token_refs[number]
        rows_ref = key_ref if number == 0 else held.at[number]

        @pl.loop(0, slab // tile)
        def _(step):
            at = pl.ds(pl.multiple_of(step * tile, tile), tile)
            value = lax.dot_general(
                token_ref[:, at], rows_ref[...], (((0,), (0,)), ((), ())),
                preferred_element_type=jnp.float32,
            )
            if number == 0:
                acc[at, :] = value
            else:
                acc[at, :] += value

    for df in range(1, fsdp):
        plane_copy(df, 0, 0).start()
    follow(0, 0, 0)
    accumulate(0, 0, 0)
    near = [(0, dy, 0) for dy in range(1, chips)] + [(df, 0, 0) for df in range(1, fsdp)]
    far = [(df, dy, 0) for df in range(1, fsdp) for dy in range(1, chips)]
    last = [(df, dy, 1) for df in range(fsdp) for dy in range(chips) if cores == 2]
    for group in (near, last[:1], far, last[1:]):
        for item in group:
            plane_copy(*item).wait_recv()
            follow(*item)
        for item in group:
            accumulate(*item)

    def part_copy(dz):
        return remote(
            ("part", dz), parts.at[dz - 1], landed.at[dz - 1], {"dp": lax.rem(z + dz, depth)}
        )

    for dz in range(1, depth):
        row = pl.multiple_of(lax.rem(z + dz, depth) * share, share)
        parts[dz - 1] = acc[pl.ds(row, share), :].astype(jnp.bfloat16)
        part_copy(dz).start()
    total = acc[pl.ds(pl.multiple_of(z * share, share), share), :]
    for dz in range(1, depth):
        part_copy(dz).wait_recv()
        total = total + landed[dz - 1].astype(jnp.float32)
    final[...] = (total * norm).astype(jnp.bfloat16)

    def rows(dy, dc, zz):
        chip = lax.rem(y - dy + chips, chips)
        core = c if dc == 0 else 1 - c
        row = ((chip * cores + core) * depth + zz) * share
        return out_ref.at[pl.ds(pl.multiple_of(row, share), share)]

    def event_depth(event):
        way, step = event
        return z if way == 0 else z - way * (step + 1)

    def event_live(event):
        where = event_depth(event)
        return (where >= 0) & (where < depth)

    def block_of(event):
        return final if event[0] == 0 else rows(0, 0, event_depth(event))

    def depth_copy(event):
        way, step = event
        where = z - way * step
        src = final if step == 0 else rows(0, 0, where)
        return remote(("z", event), src, rows(0, 0, where), {"dp": z + way})

    def depth_live(event):
        way, step = event
        where = z - way * step
        return (where >= 0) & (where < depth) & (z + way >= 0) & (z + way < depth)

    def row_copy(event, dy, dc):
        where = event_depth(event)
        if dc:
            return remote(
                ("c", event, dy), rows(dy, 0, where) if dy else block_of(event),
                rows(dy, 0, where), seq_at(0, 1),
            )
        return remote(("y", event, dy), block_of(event), rows(0, 0, where), seq_at(dy, 0))

    own = (0, 0)
    events = [own] + [(way, step) for step in range(depth - 1) for way in (1, -1)]
    own_copy = pltpu.make_async_copy(final, rows(0, 0, z), local)
    own_copy.start()

    def when(event, live, action):
        if event == own:
            action()
        else:
            pl.when(live(event))(action)

    def spread(event):
        for dy in range(1, chips):
            row_copy(event, dy, 0).start()
        if cores == 2:
            row_copy(event, 0, 1).start()

    def arrive(event):
        if event != own:
            depth_copy(event).wait_recv()
        spread(event)

    def relay(event):
        for dy in range(1, chips):
            row_copy(event, dy, 0).wait_recv()
            if cores == 2:
                row_copy(event, dy, 1).start()

    def close(event):
        for dy in range(1, chips):
            row_copy(event, dy, 0).wait_send()
        if cores == 2:
            for dy in range(chips):
                row_copy(event, dy, 1).wait()

    for way in (1, -1):
        if depth > 1:
            when((way, 0), depth_live, lambda way=way: depth_copy((way, 0)).start())
    before = None
    for event in events:
        when(event, event_live, functools.partial(arrive, event))
        if event != own and event[1] + 1 < depth - 1:
            after_it = (event[0], event[1] + 1)
            when(after_it, depth_live, lambda after_it=after_it: depth_copy(after_it).start())
        if before is not None:
            when(before, event_live, functools.partial(relay, before))
        before = event
    when(before, event_live, functools.partial(relay, before))
    for event in events:
        when(event, event_live, functools.partial(close, event))
        if event != own:
            when(event, depth_live, lambda event=event: depth_copy(event).wait_send())
    own_copy.wait()
    for df in range(fsdp):
        for dy in range(chips):
            for dc in range(cores):
                if (df, dy, dc) != (0, 0, 0):
                    plane_copy(df, dy, dc).wait_send()
    for dz in range(1, depth):
        part_copy(dz).wait_send()


def tail(key_grad, token_blocks, norm):
    fsdp, parts, depth = lax.axis_size("fsdp"), lax.axis_size("seq"), lax.axis_size("dp")
    cores = pair_count(parts)
    chips = parts // cores
    count = len(token_blocks)
    rows, slab = token_blocks[0].shape
    width = key_grad.shape[1]
    share = slab // depth
    copies = count - 1 + depth - 1 + 2 * (depth - 1) + (2 * depth - 1) * (chips - 1 + chips)
    return pl.pallas_call(
        functools.partial(tail_kernel, fsdp, chips, cores, depth, share, norm),
        out_shape=jax.ShapeDtypeStruct((slab * parts, width), jnp.bfloat16),
        in_specs=[pl.BlockSpec(memory_space=pltpu.VMEM)] * (1 + count),
        out_specs=pl.BlockSpec(memory_space=pl.ANY),
        scratch_shapes=[
            pltpu.VMEM((count, rows, width), jnp.bfloat16),
            pltpu.VMEM((slab, width), jnp.float32),
            pltpu.VMEM((max(depth - 1, 1), share, width), jnp.bfloat16),
            pltpu.VMEM((max(depth - 1, 1), share, width), jnp.bfloat16),
            pltpu.VMEM((share, width), jnp.bfloat16),
            pltpu.SemaphoreType.DMA((copies,)),
            pltpu.SemaphoreType.DMA((copies,)),
            pltpu.SemaphoreType.DMA(()),
        ],
        compiler_params=pltpu.CompilerParams(collective_id=0, has_side_effects=True),
        name="tail",
    )(key_grad, *token_blocks)


def project_kernel(fsdp, chips, cores, chunks, token_hbm, weight_hbm, ext_ref, *scratch):
    tokens, weight, gathered, acc, key_out, before, send, recv, local = scratch
    parts = chips * cores
    rows = tokens.shape[0]
    shard = weight.shape[0]
    slab = shard // parts
    chunk = slab // chunks
    f, s = lax.axis_index("fsdp"), lax.axis_index("seq")
    y, c = lax.div(s, cores), lax.rem(s, cores)

    def seq_of(dy, dc):
        other = c if dc == 0 else 1 - c
        return lax.rem(y + dy + chips, chips) * cores + other

    partners = [{"fsdp": lax.rem(f + df, fsdp)} for df in range(1, fsdp)]
    partners += [{"seq": seq_of(dy, 0)} for dy in range(1, chips)]
    partners += [{"seq": seq_of(0, 1)}] * (cores - 1)
    if parts > 1:
        partners += [{"seq": lax.rem(s + 1, parts)}, {"seq": lax.rem(s + parts - 1, parts)}]
    barrier = pltpu.get_barrier_semaphore()
    for device in partners:
        pl.semaphore_signal(barrier, inc=1, device_id=device, device_id_type=MESH)
    token_copy = pltpu.make_async_copy(token_hbm, tokens, local.at[0])
    weight_copy = pltpu.make_async_copy(weight_hbm, weight, local.at[1])
    token_copy.start()
    weight_copy.start()
    pl.semaphore_wait(barrier, len(partners))

    numbers = {}

    def remote(name, src, dst, device):
        slot = numbers.setdefault(name, len(numbers))
        return pltpu.make_async_remote_copy(
            src_ref=src,
            dst_ref=dst,
            send_sem=send.at[slot],
            recv_sem=recv.at[slot],
            device_id=device,
            device_id_type=MESH,
        )

    def span(owner, k, count=1):
        return pl.ds(pl.multiple_of(owner * slab + k * chunk, chunk), count * chunk)

    def first(df, k):
        at = span(s, k)
        return remote(
            (df, k), weight_hbm.at[at], gathered.at[df - 1, at], {"fsdp": lax.rem(f + df, fsdp)}
        )

    def along(df, k, dy):
        at = span(s, k)
        piece = gathered.at[df - 1, at]
        return remote((df, k, "y", dy), piece, piece, {"seq": seq_of(dy, 0)})

    def across(df, k, dy):
        at = span(seq_of(-dy, 0), k)
        piece = gathered.at[df - 1, at]
        return remote((df, k, "c", dy), piece, piece, {"seq": seq_of(0, 1)})

    shards_in = range(1, fsdp)
    for k in range(chunks):
        for df in shards_in:
            first(df, k).start()
    token_copy.wait()
    weight_copy.wait()
    step = shard // chunks
    group = 2 if chunks % 2 == 0 else 1

    def own_part(k):
        at = pl.ds(pl.multiple_of(f * shard + k * step, step), step)
        value = jnp.dot(
            tokens[:, at], weight[k * step : (k + 1) * step, :],
            preferred_element_type=jnp.float32,
        )
        if k == 0:
            acc[...] = value
        else:
            acc[...] += value

    def landed(k):
        for df in shards_in:
            first(df, k).wait_recv()
            for dy in range(1, chips):
                along(df, k, dy).start()
            if cores == 2:
                across(df, k, 0).start()

    def passed(k):
        for df in shards_in:
            for dy in range(1, chips):
                along(df, k, dy).wait_recv()
                if cores == 2:
                    across(df, k, dy).start()

    def used(k):
        if cores == 2:
            for df in shards_in:
                for dy in range(chips):
                    across(df, k, dy).wait_recv()
        if (k + 1) % group == 0:
            begin = k + 1 - group
            for df in shards_in:
                owner = lax.rem(f - df + fsdp, fsdp) * shard
                value = None
                for dy in range(chips):
                    for dc in range(cores):
                        holder = seq_of(-dy, dc)
                        columns = owner + holder * slab + begin * chunk
                        at = pl.ds(pl.multiple_of(columns, group * chunk), group * chunk)
                        term = jnp.dot(
                            tokens[:, at], gathered[df - 1, span(holder, begin, group), :],
                            preferred_element_type=jnp.float32,
                        )
                        value = term if value is None else value + term
                acc[...] += value

    for k in range(chunks + 2):
        if k < chunks:
            own_part(k)
            landed(k)
        if 1 <= k <= chunks:
            passed(k - 1)
        if k >= 2:
            used(k - 2)

    key_out[...] = acc[...].astype(key_out.dtype)
    halo = remote("halo", key_out, before, {"seq": lax.rem(s + 1, parts)})

    @pl.when(s + 1 < parts)
    def _():
        halo.start()

    ext_ref[rows:, :] = key_out[...]

    @pl.when(s == 0)
    def _():
        ext_ref[:rows, :] = jnp.zeros_like(key_out)

    @pl.when(s > 0)
    def _():
        halo.wait_recv()
        ext_ref[:rows, :] = before[...]

    @pl.when(s + 1 < parts)
    def _():
        halo.wait_send()

    for k in range(chunks):
        for df in shards_in:
            first(df, k).wait_send()
            for dy in range(1, chips):
                along(df, k, dy).wait_send()
            if cores == 2:
                for dy in range(chips):
                    across(df, k, dy).wait_send()


def project(tokens, key_weight):
    fsdp, parts = lax.axis_size("fsdp"), lax.axis_size("seq")
    cores = pair_count(parts)
    chips = parts // cores
    rows = tokens.shape[0]
    shard, width = key_weight.shape
    chunks = max(1, min(8, shard // parts // 128))
    copies = (fsdp - 1) * chunks * (1 + chips - 1 + chips) + 1
    return pl.pallas_call(
        functools.partial(project_kernel, fsdp, chips, cores, chunks),
        out_shape=jax.ShapeDtypeStruct((2 * rows, width), jnp.bfloat16),
        in_specs=[pl.BlockSpec(memory_space=pl.ANY)] * 2,
        out_specs=pl.BlockSpec(memory_space=pltpu.VMEM),
        scratch_shapes=[
            pltpu.VMEM(tokens.shape, tokens.dtype),
            pltpu.VMEM(key_weight.shape, key_weight.dtype),
            pltpu.VMEM((max(fsdp - 1, 1), shard, width), key_weight.dtype),
            pltpu.VMEM((rows, width), jnp.float32),
            pltpu.VMEM((rows, width), jnp.bfloat16),
            pltpu.VMEM((rows, width), jnp.bfloat16),
            pltpu.SemaphoreType.DMA((copies,)),
            pltpu.SemaphoreType.DMA((copies,)),
            pltpu.SemaphoreType.DMA((2,)),
        ],
        compiler_params=pltpu.CompilerParams(collective_id=1, has_side_effects=True),
        name="project",
    )(tokens, key_weight)


def shards(queries, hidden, key_weight, doc_lengths, entropy_cot):
    tokens = hidden[0]
    local_rows, width = tokens.shape
    seq_parts = lax.axis_size("seq")
    fsdp_parts = lax.axis_size("fsdp")
    dp_parts = lax.axis_size("dp")
    cores = pair_count(seq_parts)
    chips = seq_parts // cores
    f_pos, s_pos = lax.axis_index("fsdp"), lax.axis_index("seq")
    y_pos, c_pos = s_pos // cores, s_pos % cores
    shard_rows = width // fsdp_parts
    slab = shard_rows // seq_parts
    seq_len = local_rows * seq_parts
    group_size = QH // KVH
    doc_index = document_index(doc_lengths[0], seq_len)

    def seq_at(dy, dc):
        return ((y_pos + dy) % chips) * cores + (c_pos ^ dc)

    def column_slab(f, s, start, count):
        return lax.dynamic_slice_in_dim(tokens, f * shard_rows + s * slab + start, count, 1)

    ext_keys = project(tokens, key_weight)

    plane = [
        (df, dy, dc) for df in range(fsdp_parts) for dy in range(chips) for dc in range(cores)
    ]
    token_blocks = []
    for df, dy, dc in plane:
        block = column_slab((f_pos + df) % fsdp_parts, seq_at(dy, dc), 0, slab)
        if (df, dy, dc) != (0, 0, 0):
            block = after(block, ext_keys)
            block = shift_plane(block, df, dy, dc)
        token_blocks.append(block)

    query_local = queries[0]
    cot_local = entropy_cot[0]
    start = s_pos * local_rows
    prev_index = lax.dynamic_slice_in_dim(
        doc_index, jnp.maximum(start - local_rows, 0), local_rows, 0
    )
    prev_index = jnp.where(s_pos > 0, prev_index, -1)
    own_index = lax.dynamic_slice_in_dim(doc_index, start, local_rows, 0)
    ext_index = jnp.concatenate([prev_index, own_index], axis=0)
    ext_keys = ext_keys.reshape(2 * local_rows, KVH, HD)
    entropy_heads, grad_heads, key_heads_ext = per_head(
        query_local.reshape(local_rows, KVH, group_size, HD),
        ext_keys,
        cot_local.reshape(local_rows, KVH, group_size),
        ext_index,
        local_rows,
        local_rows,
    )
    entropy_local = entropy_heads.reshape(local_rows, QH)
    grad_local = grad_heads.reshape(local_rows, QH * HD)
    key_ext = key_heads_ext.reshape(2 * local_rows, KVH * HD)
    returned = from_behind(key_ext[:local_rows], "seq", -1)
    key_grad = (key_ext[local_rows:] + returned).astype(jnp.bfloat16)

    token_blocks = [after(block, key_grad) for block in token_blocks]

    norm_factor = (seq_len * fsdp_parts * dp_parts) ** (-0.5)
    grad_local = grad_local.astype(jnp.bfloat16)
    key_grad, entropy_local, grad_local = lax.optimization_barrier(
        (key_grad, entropy_local, grad_local)
    )
    weight_grad = tail(key_grad, token_blocks, norm_factor)
    return (
        entropy_local.reshape(1, local_rows, QH),
        grad_local.reshape(1, local_rows, QH * HD),
        weight_grad,
    )


def solution(mesh):
    return jax.shard_map(
        shards,
        mesh=mesh,
        in_specs=(
            P(("fsdp", "dp"), "seq", None),
            P(("fsdp", "dp"), "seq", None),
            P("fsdp", None),
            P(("fsdp", "dp"), None),
            P(("fsdp", "dp"), "seq", None),
        ),
        out_specs=(P(("fsdp", "dp"), "seq", None), P(("fsdp", "dp"), "seq", None), P("fsdp", None)),
        check_vma=False,
    )
```

```python
import functools

import jax
import jax.numpy as jnp
from jax import lax
from jax.experimental import pallas as pl
from jax.experimental.pallas import tpu as pltpu
from jax.sharding import PartitionSpec as P


QH = 32
KVH = 4
HD = 128


def from_behind(shard, axis, by):
    length = lax.axis_size(axis)
    pairs = [(i, i + by) for i in range(length) if 0 <= i + by < length]
    return lax.ppermute(shard, axis, pairs)


def document_index(lengths, seq_len):
    ends = jnp.cumsum(lengths)
    position = jnp.arange(seq_len, dtype=jnp.int32)
    return jnp.sum((ends[None, :] <= position[:, None]).astype(jnp.int32), axis=1)


def attend(queries, key_rows, cotangent, doc_index, anchor, doc_len):
    row_count, key_heads, group_size, head_size = queries.shape
    full_len = key_rows.shape[0]
    block_rows = min(512, row_count)
    window = block_rows + doc_len
    factor = head_size ** (-0.5)
    keys_padded = jnp.concatenate(
        [jnp.zeros((doc_len, key_heads, head_size), key_rows.dtype), key_rows], axis=0
    )
    index_padded = jnp.concatenate([jnp.full((doc_len,), -1, jnp.int32), doc_index], axis=0)

    def one_block(step_index, state_now):
        entropy, grad_query, grad_key = state_now
        row_start = (step_index * block_rows).astype(jnp.int32)
        position = anchor + row_start
        weight_block = cotangent.astype(jnp.float32)
        key_block = lax.dynamic_slice_in_dim(keys_padded, position, window, 0)
        key_docs = lax.dynamic_slice_in_dim(index_padded, position, window, 0)
        query_docs = lax.dynamic_slice_in_dim(doc_index, position, block_rows, 0)
        query_pos = position + jnp.arange(block_rows, dtype=jnp.int32)
        key_pos = position - doc_len + jnp.arange(window, dtype=jnp.int32)
        visible = (query_docs[:, None] == key_docs[None, :]) & (
            key_pos[None, :] <= query_pos[:, None]
        )
        scores = (
            jnp.einsum("rkgd,wkd->kgrw", queries, key_block, preferred_element_type=jnp.float32)
            * factor
        )
        scores = jnp.where(visible, scores, -1e30)
        row_max = jnp.max(scores, axis=-1, keepdims=True)
        powers = jnp.exp(scores - row_max)
        denominator = jnp.sum(powers, axis=-1, keepdims=True)
        probability = powers / denominator
        mean_score = jnp.sum(jnp.where(visible, probability * scores, 0.0), axis=-1, keepdims=True)
        block_entropy = (row_max + jnp.log(denominator) - mean_score)[..., 0]
        row_weight = jnp.transpose(weight_block, (1, 2, 0))[..., None]
        slope = jnp.where(visible, row_weight * probability * (mean_score - scores), 0.0).astype(
            jnp.bfloat16
        )
        query_part = (
            jnp.einsum("kgrw,wkd->rkgd", slope, key_block, preferred_element_type=jnp.float32)
            * factor
        )
        key_part = (
            jnp.einsum("kgrw,rkgd->wkd", slope, queries, preferred_element_type=jnp.float32)
            * factor
        )
        entropy = jnp.transpose(block_entropy, (2, 0, 1))
        grad_query = query_part
        previous = lax.dynamic_slice_in_dim(grad_key, position, window, 0)
        grad_key = lax.dynamic_update_slice_in_dim(grad_key, previous + key_part, position, 0)
        return (entropy, grad_query, grad_key)

    initial = (
        jnp.zeros((row_count, key_heads, group_size), jnp.float32),
        jnp.zeros((row_count, key_heads, group_size, head_size), jnp.float32),
        jnp.zeros((full_len + doc_len, key_heads, head_size), jnp.float32),
    )
    entropy, grad_query, grad_key = lax.fori_loop(0, row_count // block_rows, one_block, initial)
    return (entropy, grad_query, grad_key[doc_len:])


def per_head(query_four, key_rows, cot_three, doc_index, anchor, doc_len):
    outcome = [
        attend(
            query_four[:, head_index : head_index + 1],
            key_rows[:, head_index : head_index + 1],
            cot_three[:, head_index : head_index + 1],
            doc_index,
            anchor,
            doc_len,
        )
        for head_index in range(query_four.shape[1])
    ]
    entropy = jnp.concatenate([item_set[0] for item_set in outcome], axis=1)
    grad_query = jnp.concatenate([item_set[1] for item_set in outcome], axis=1)
    grad_key = jnp.concatenate([item_set[2] for item_set in outcome], axis=1)
    return (entropy, grad_query, grad_key)


def after(value, *earlier):
    return lax.optimization_barrier((value, *earlier))[0]


def pair_count(seq_parts):
    return 2 if seq_parts % 2 == 0 else 1


def shift_plane(value, df, dy, dc):
    fsdp, parts = lax.axis_size("fsdp"), lax.axis_size("seq")
    cores = pair_count(parts)
    chips = parts // cores
    pairs = [
        ((y * cores + c) * fsdp + f, (((y + dy) % chips) * cores + (c ^ dc)) * fsdp + (f + df) % fsdp)
        for f in range(fsdp)
        for y in range(chips)
        for c in range(cores)
    ]
    return lax.ppermute(value, ("seq", "fsdp"), pairs)


MESH = pl.DeviceIdType.MESH


def tail_kernel(fsdp, chips, cores, depth, share, norm, *refs):
    count = fsdp * chips * cores
    key_ref, token_refs, out_ref = refs[0], refs[1 : 1 + count], refs[1 + count]
    held, acc, parts, landed, final, send, recv, local = refs[2 + count :]
    slab = depth * share
    f, s, z = lax.axis_index("fsdp"), lax.axis_index("seq"), lax.axis_index("dp")
    y, c = lax.div(s, cores), lax.rem(s, cores)

    def seq_at(dy, dc):
        other = c if dc == 0 else 1 - c
        return {"seq": lax.rem(y + dy + chips, chips) * cores + other}

    def fsdp_at(df):
        return {"fsdp": lax.rem(f + df, fsdp)}

    partners = [fsdp_at(df) for df in range(1, fsdp)]
    partners += [seq_at(dy, 0) for dy in range(1, chips)]
    partners += [seq_at(0, 1)] * (cores - 1)
    partners += [{"dp": lax.rem(z + dz, depth)} for dz in range(1, depth)]
    barrier = pltpu.get_barrier_semaphore()
    for device in partners:
        pl.semaphore_signal(barrier, inc=1, device_id=device, device_id_type=MESH)
    pl.semaphore_wait(barrier, len(partners))

    numbers = {}

    def remote(name, src, dst, device):
        slot = numbers.setdefault(name, len(numbers))
        return pltpu.make_async_remote_copy(
            src_ref=src,
            dst_ref=dst,
            send_sem=send.at[slot],
            recv_sem=recv.at[slot],
            device_id=device,
            device_id_type=MESH,
        )

    def place(df, dy, dc):
        return (df * chips + dy) * cores + dc

    def plane_copy(df, dy, dc):
        if dc:
            source, device = (df, dy, 0), seq_at(0, 1)
        elif dy:
            source, device = (df, 0, 0), seq_at(dy, 0)
        else:
            source, device = (0, 0, 0), fsdp_at(df)
        src = key_ref if source == (0, 0, 0) else held.at[place(*source)]
        return remote(("key", df, dy, dc), src, held.at[place(df, dy, dc)], device)

    def follow(df, dy, dc):
        if dc == 0:
            if dy == 0:
                for step in range(1, chips):
                    plane_copy(df, step, 0).start()
            if cores == 2:
                plane_copy(df, dy, 1).start()

    tile = min(256, slab)

    def accumulate(df, dy, dc):
        number = place(df, dy, dc)
        token_ref = token_refs[number]
        rows_ref = key_ref if number == 0 else held.at[number]

        @pl.loop(0, slab // tile)
        def _(step):
            at = pl.ds(pl.multiple_of(step * tile, tile), tile)
            value = lax.dot_general(
                token_ref[:, at], rows_ref[...], (((0,), (0,)), ((), ())),
                preferred_element_type=jnp.float32,
            )
            if number == 0:
                acc[at, :] = value
            else:
                acc[at, :] += value

    for df in range(1, fsdp):
        plane_copy(df, 0, 0).start()
    follow(0, 0, 0)
    accumulate(0, 0, 0)
    near = [(0, dy, 0) for dy in range(1, chips)] + [(df, 0, 0) for df in range(1, fsdp)]
    far = [(df, dy, 0) for df in range(1, fsdp) for dy in range(1, chips)]
    last = [(df, dy, 1) for df in range(fsdp) for dy in range(chips) if cores == 2]
    for group in (near, last[:1], far, last[1:]):
        for item in group:
            plane_copy(*item).wait_recv()
            follow(*item)
        for item in group:
            accumulate(*item)

    halves = final.shape[0]
    piece = share // halves

    def part_copy(dz, h):
        return remote(
            ("part", dz, h), parts.at[h, dz - 1], landed.at[h, dz - 1],
            {"dp": lax.rem(z + dz, depth)},
        )

    for h in range(halves):
        for dz in range(1, depth):
            row = pl.multiple_of(lax.rem(z + dz, depth) * share + h * piece, piece)
            parts[h, dz - 1] = acc[pl.ds(row, piece), :].astype(jnp.bfloat16)
            part_copy(dz, h).start()

    def rows(dy, dc, zz, h):
        chip = lax.rem(y - dy + chips, chips)
        core = c if dc == 0 else 1 - c
        row = ((chip * cores + core) * depth + zz) * share + h * piece
        return out_ref.at[pl.ds(pl.multiple_of(row, piece), piece)]

    def event_depth(event):
        way, step, _ = event
        return z if way == 0 else z - way * (step + 1)

    def event_live(event):
        where = event_depth(event)
        return (where >= 0) & (where < depth)

    def block_of(event):
        h = event[2]
        return final.at[h] if event[0] == 0 else rows(0, 0, event_depth(event), h)

    def depth_copy(event):
        way, step, h = event
        where = z - way * step
        src = final.at[h] if step == 0 else rows(0, 0, where, h)
        return remote(("z", event), src, rows(0, 0, where, h), {"dp": z + way})

    def depth_live(event):
        way, step, _ = event
        where = z - way * step
        return (where >= 0) & (where < depth) & (z + way >= 0) & (z + way < depth)

    def row_copy(event, dy, dc):
        where, h = event_depth(event), event[2]
        if dc:
            return remote(
                ("c", event, dy), rows(dy, 0, where, h) if dy else block_of(event),
                rows(dy, 0, where, h), seq_at(0, 1),
            )
        return remote(("y", event, dy), block_of(event), rows(0, 0, where, h), seq_at(dy, 0))

    events = [(0, 0, h) for h in range(halves)]
    for step in range(depth - 1):
        events += [(way, step, h) for h in range(halves) for way in (1, -1)]

    def own_copy(h):
        return pltpu.make_async_copy(final.at[h], rows(0, 0, z, h), local.at[h])

    def when(event, live, action):
        if event[0] == 0:
            action()
        else:
            pl.when(live(event))(action)

    def finish_sum(h):
        total = acc[pl.ds(pl.multiple_of(z * share + h * piece, piece), piece), :]
        for dz in range(1, depth):
            part_copy(dz, h).wait_recv()
            total = total + landed[h, dz - 1].astype(jnp.float32)
        final[h] = (total * norm).astype(jnp.bfloat16)
        own_copy(h).start()
        if depth > 1:
            for way in (1, -1):
                first = (way, 0, h)
                when(first, depth_live, lambda first=first: depth_copy(first).start())

    def arrive(event):
        if event[0] == 0:
            finish_sum(event[2])
        else:
            depth_copy(event).wait_recv()
        for dy in range(1, chips):
            row_copy(event, dy, 0).start()
        if cores == 2:
            row_copy(event, 0, 1).start()

    def relay(event):
        for dy in range(1, chips):
            row_copy(event, dy, 0).wait_recv()
            if cores == 2:
                row_copy(event, dy, 1).start()

    def close(event):
        for dy in range(1, chips):
            row_copy(event, dy, 0).wait_send()
        if cores == 2:
            for dy in range(chips):
                row_copy(event, dy, 1).wait()

    waiting = []
    for event in events:
        when(event, event_live, functools.partial(arrive, event))
        way, step, h = event
        if way != 0 and step + 1 < depth - 1:
            onward = (way, step + 1, h)
            when(onward, depth_live, lambda onward=onward: depth_copy(onward).start())
        waiting.append(event)
        if len(waiting) > 2:
            when(waiting[0], event_live, functools.partial(relay, waiting[0]))
            waiting.pop(0)
    for event in waiting:
        when(event, event_live, functools.partial(relay, event))
    for event in events:
        when(event, event_live, functools.partial(close, event))
        if event[0] != 0:
            when(event, depth_live, lambda event=event: depth_copy(event).wait_send())
        else:
            own_copy(event[2]).wait()
    for df in range(fsdp):
        for dy in range(chips):
            for dc in range(cores):
                if (df, dy, dc) != (0, 0, 0):
                    plane_copy(df, dy, dc).wait_send()
    for h in range(halves):
        for dz in range(1, depth):
            part_copy(dz, h).wait_send()


def tail(key_grad, token_blocks, norm):
    fsdp, parts, depth = lax.axis_size("fsdp"), lax.axis_size("seq"), lax.axis_size("dp")
    cores = pair_count(parts)
    chips = parts // cores
    count = len(token_blocks)
    rows, slab = token_blocks[0].shape
    width = key_grad.shape[1]
    share = slab // depth
    halves = 2 if share % 32 == 0 else 1
    copies = depth - 1 + 2 * (depth - 1) + (2 * depth - 1) * (chips - 1 + chips)
    copies = count - 1 + halves * copies
    pieces = pltpu.VMEM((halves, max(depth - 1, 1), share // halves, width), jnp.bfloat16)
    return pl.pallas_call(
        functools.partial(tail_kernel, fsdp, chips, cores, depth, share, norm),
        out_shape=jax.ShapeDtypeStruct((slab * parts, width), jnp.bfloat16),
        in_specs=[pl.BlockSpec(memory_space=pltpu.VMEM)] * (1 + count),
        out_specs=pl.BlockSpec(memory_space=pl.ANY),
        scratch_shapes=[
            pltpu.VMEM((count, rows, width), jnp.bfloat16),
            pltpu.VMEM((slab, width), jnp.float32),
            pieces,
            pieces,
            pltpu.VMEM((halves, share // halves, width), jnp.bfloat16),
            pltpu.SemaphoreType.DMA((copies,)),
            pltpu.SemaphoreType.DMA((copies,)),
            pltpu.SemaphoreType.DMA((halves,)),
        ],
        compiler_params=pltpu.CompilerParams(collective_id=0, has_side_effects=True),
        name="tail",
    )(key_grad, *token_blocks)


def project_kernel(fsdp, chips, cores, chunks, token_hbm, weight_hbm, ext_ref, *scratch):
    tokens, weight, gathered, acc, key_out, before, send, recv, local = scratch
    parts = chips * cores
    rows = tokens.shape[0]
    shard = weight.shape[0]
    slab = shard // parts
    chunk = slab // chunks
    f, s = lax.axis_index("fsdp"), lax.axis_index("seq")
    y, c = lax.div(s, cores), lax.rem(s, cores)

    def seq_of(dy, dc):
        other = c if dc == 0 else 1 - c
        return lax.rem(y + dy + chips, chips) * cores + other

    partners = [{"fsdp": lax.rem(f + df, fsdp)} for df in range(1, fsdp)]
    partners += [{"seq": seq_of(dy, 0)} for dy in range(1, chips)]
    partners += [{"seq": seq_of(0, 1)}] * (cores - 1)
    if parts > 1:
        partners += [{"seq": lax.rem(s + 1, parts)}, {"seq": lax.rem(s + parts - 1, parts)}]
    barrier = pltpu.get_barrier_semaphore()
    for device in partners:
        pl.semaphore_signal(barrier, inc=1, device_id=device, device_id_type=MESH)
    token_copy = pltpu.make_async_copy(token_hbm, tokens, local.at[0])
    weight_copy = pltpu.make_async_copy(weight_hbm, weight, local.at[1])
    token_copy.start()
    weight_copy.start()
    pl.semaphore_wait(barrier, len(partners))

    numbers = {}

    def remote(name, src, dst, device):
        slot = numbers.setdefault(name, len(numbers))
        return pltpu.make_async_remote_copy(
            src_ref=src,
            dst_ref=dst,
            send_sem=send.at[slot],
            recv_sem=recv.at[slot],
            device_id=device,
            device_id_type=MESH,
        )

    def span(owner, k, count=1):
        return pl.ds(pl.multiple_of(owner * slab + k * chunk, chunk), count * chunk)

    def first(df, k):
        at = span(s, k)
        return remote(
            (df, k), weight_hbm.at[at], gathered.at[df - 1, at], {"fsdp": lax.rem(f + df, fsdp)}
        )

    def along(df, k, dy):
        at = span(s, k)
        piece = gathered.at[df - 1, at]
        return remote((df, k, "y", dy), piece, piece, {"seq": seq_of(dy, 0)})

    def across(df, k, dy):
        at = span(seq_of(-dy, 0), k)
        piece = gathered.at[df - 1, at]
        return remote((df, k, "c", dy), piece, piece, {"seq": seq_of(0, 1)})

    shards_in = range(1, fsdp)
    for k in range(chunks):
        for df in shards_in:
            first(df, k).start()
    token_copy.wait()
    weight_copy.wait()
    step = shard // chunks
    group = 2 if chunks % 2 == 0 else 1

    def own_part(k):
        at = pl.ds(pl.multiple_of(f * shard + k * step, step), step)
        value = jnp.dot(
            tokens[:, at], weight[k * step : (k + 1) * step, :],
            preferred_element_type=jnp.float32,
        )
        if k == 0:
            acc[...] = value
        else:
            acc[...] += value

    def landed(k):
        for df in shards_in:
            first(df, k).wait_recv()
            for dy in range(1, chips):
                along(df, k, dy).start()
            if cores == 2:
                across(df, k, 0).start()

    def passed(k):
        for df in shards_in:
            for dy in range(1, chips):
                along(df, k, dy).wait_recv()
                if cores == 2:
                    across(df, k, dy).start()

    def used(k):
        if cores == 2:
            for df in shards_in:
                for dy in range(chips):
                    across(df, k, dy).wait_recv()
        if (k + 1) % group == 0:
            begin = k + 1 - group
            for df in shards_in:
                owner = lax.rem(f - df + fsdp, fsdp) * shard
                value = None
                for dy in range(chips):
                    for dc in range(cores):
                        holder = seq_of(-dy, dc)
                        columns = owner + holder * slab + begin * chunk
                        at = pl.ds(pl.multiple_of(columns, group * chunk), group * chunk)
                        term = jnp.dot(
                            tokens[:, at], gathered[df - 1, span(holder, begin, group), :],
                            preferred_element_type=jnp.float32,
                        )
                        value = term if value is None else value + term
                acc[...] += value

    for k in range(chunks + 2):
        if k < chunks:
            own_part(k)
            landed(k)
        if 1 <= k <= chunks:
            passed(k - 1)
        if k >= 2:
            used(k - 2)

    key_out[...] = acc[...].astype(key_out.dtype)
    halo = remote("halo", key_out, before, {"seq": lax.rem(s + 1, parts)})

    @pl.when(s + 1 < parts)
    def _():
        halo.start()

    ext_ref[rows:, :] = key_out[...]

    @pl.when(s == 0)
    def _():
        ext_ref[:rows, :] = jnp.zeros_like(key_out)

    @pl.when(s > 0)
    def _():
        halo.wait_recv()
        ext_ref[:rows, :] = before[...]

    @pl.when(s + 1 < parts)
    def _():
        halo.wait_send()

    for k in range(chunks):
        for df in shards_in:
            first(df, k).wait_send()
            for dy in range(1, chips):
                along(df, k, dy).wait_send()
            if cores == 2:
                for dy in range(chips):
                    across(df, k, dy).wait_send()


def project(tokens, key_weight):
    fsdp, parts = lax.axis_size("fsdp"), lax.axis_size("seq")
    cores = pair_count(parts)
    chips = parts // cores
    rows = tokens.shape[0]
    shard, width = key_weight.shape
    chunks = max(1, min(8, shard // parts // 128))
    copies = (fsdp - 1) * chunks * (1 + chips - 1 + chips) + 1
    return pl.pallas_call(
        functools.partial(project_kernel, fsdp, chips, cores, chunks),
        out_shape=jax.ShapeDtypeStruct((2 * rows, width), jnp.bfloat16),
        in_specs=[pl.BlockSpec(memory_space=pl.ANY)] * 2,
        out_specs=pl.BlockSpec(memory_space=pltpu.VMEM),
        scratch_shapes=[
            pltpu.VMEM(tokens.shape, tokens.dtype),
            pltpu.VMEM(key_weight.shape, key_weight.dtype),
            pltpu.VMEM((max(fsdp - 1, 1), shard, width), key_weight.dtype),
            pltpu.VMEM((rows, width), jnp.float32),
            pltpu.VMEM((rows, width), jnp.bfloat16),
            pltpu.VMEM((rows, width), jnp.bfloat16),
            pltpu.SemaphoreType.DMA((copies,)),
            pltpu.SemaphoreType.DMA((copies,)),
            pltpu.SemaphoreType.DMA((2,)),
        ],
        compiler_params=pltpu.CompilerParams(collective_id=1, has_side_effects=True),
        name="project",
    )(tokens, key_weight)


def shards(queries, hidden, key_weight, doc_lengths, entropy_cot):
    tokens = hidden[0]
    local_rows, width = tokens.shape
    seq_parts = lax.axis_size("seq")
    fsdp_parts = lax.axis_size("fsdp")
    dp_parts = lax.axis_size("dp")
    cores = pair_count(seq_parts)
    chips = seq_parts // cores
    f_pos, s_pos = lax.axis_index("fsdp"), lax.axis_index("seq")
    y_pos, c_pos = s_pos // cores, s_pos % cores
    shard_rows = width // fsdp_parts
    slab = shard_rows // seq_parts
    seq_len = local_rows * seq_parts
    group_size = QH // KVH
    doc_index = document_index(doc_lengths[0], seq_len)

    def seq_at(dy, dc):
        return ((y_pos + dy) % chips) * cores + (c_pos ^ dc)

    def column_slab(f, s, start, count):
        return lax.dynamic_slice_in_dim(tokens, f * shard_rows + s * slab + start, count, 1)

    ext_keys = project(tokens, key_weight)

    plane = [
        (df, dy, dc) for df in range(fsdp_parts) for dy in range(chips) for dc in range(cores)
    ]
    token_blocks = []
    for df, dy, dc in plane:
        block = column_slab((f_pos + df) % fsdp_parts, seq_at(dy, dc), 0, slab)
        if (df, dy, dc) != (0, 0, 0):
            block = after(block, ext_keys)
            block = shift_plane(block, df, dy, dc)
        token_blocks.append(block)

    query_local = queries[0]
    cot_local = entropy_cot[0]
    start = s_pos * local_rows
    prev_index = lax.dynamic_slice_in_dim(
        doc_index, jnp.maximum(start - local_rows, 0), local_rows, 0
    )
    prev_index = jnp.where(s_pos > 0, prev_index, -1)
    own_index = lax.dynamic_slice_in_dim(doc_index, start, local_rows, 0)
    ext_index = jnp.concatenate([prev_index, own_index], axis=0)
    ext_keys = ext_keys.reshape(2 * local_rows, KVH, HD)
    entropy_heads, grad_heads, key_heads_ext = per_head(
        query_local.reshape(local_rows, KVH, group_size, HD),
        ext_keys,
        cot_local.reshape(local_rows, KVH, group_size),
        ext_index,
        local_rows,
        local_rows,
    )
    entropy_local = entropy_heads.reshape(local_rows, QH)
    grad_local = grad_heads.reshape(local_rows, QH * HD)
    key_ext = key_heads_ext.reshape(2 * local_rows, KVH * HD)
    returned = from_behind(key_ext[:local_rows], "seq", -1)
    key_grad = (key_ext[local_rows:] + returned).astype(jnp.bfloat16)

    token_blocks = [after(block, key_grad) for block in token_blocks]

    norm_factor = (seq_len * fsdp_parts * dp_parts) ** (-0.5)
    grad_local = grad_local.astype(jnp.bfloat16)
    key_grad, entropy_local, grad_local = lax.optimization_barrier(
        (key_grad, entropy_local, grad_local)
    )
    weight_grad = tail(key_grad, token_blocks, norm_factor)
    return (
        entropy_local.reshape(1, local_rows, QH),
        grad_local.reshape(1, local_rows, QH * HD),
        weight_grad,
    )


def solution(mesh):
    return jax.shard_map(
        shards,
        mesh=mesh,
        in_specs=(
            P(("fsdp", "dp"), "seq", None),
            P(("fsdp", "dp"), "seq", None),
            P("fsdp", None),
            P(("fsdp", "dp"), None),
            P(("fsdp", "dp"), "seq", None),
        ),
        out_specs=(P(("fsdp", "dp"), "seq", None), P(("fsdp", "dp"), "seq", None), P("fsdp", None)),
        check_vma=False,
    )
```
